32 devices in a mesh: blk: 4 (over z), uly: 8 (over y, x, core).
Axes of the slice: x: 2, y: 2, z: 4, core: 2. Of those that a mesh axis runs over, the one named last changes fastest.
Arguments:
- queries: bfloat16 [4096, 4096], P(('blk', 'uly')), may hold values from -6 to 6
- keys: bfloat16 [4096, 1024], P(('blk', 'uly')), may hold values from -6 to 6
- values: bfloat16 [4096, 1024], P(('blk', 'uly')), may hold values from -6 to 6
- grad_out: bfloat16 [4096, 4096], P(('blk', 'uly')), may hold values from -6 to 6
- row_delta: float32 [4096, 32], P(('blk', 'uly')), may hold values from -18 to 18
- doc_ids: int32 [4096], replicated, may hold values from 0 to 63, never falling along the last dimension, each value on 1 to 128 neighbouring positions
- doc_lang: int32 [64], replicated, may hold values from 0 to 3
- tile_list: int32 [8, 32, 2], replicated, may hold values from 0 to 31, as said below
Outputs:
- grad_queries: bfloat16 [4096, 4096], P(('blk', 'uly'))
- grad_keys: bfloat16 [4096, 1024], P(('blk', 'uly'))
- grad_values: bfloat16 [4096, 1024], P(('blk', 'uly'))
The draws below stay inside these ranges and needn't reach their ends.
Inputs may be any that keep to these rules, and one draw needn't show every extreme that they name: `doc_ids`: document ids never fall, rise by one where a new document begins, and a document holds at most 128 tokens. `tile_list`: each listed tile of query tile a is at most a and not before the first tile of the block of 8 tiles that precedes the block of a; entries may repeat.
All inputs are finite; a program needn't handle non-finite values.
Results may differ from the reference program's by a relative error of at most 0.0059.
Values may be sent and summed in bfloat16 or wider, within the bound.
A program may use at most 128 MiB of HBM per device.

```python
import math
import jax
import jax.numpy as jnp
import numpy as np
from jax import lax

H = 32
DH = 128
G = 8
BLOCK = 128
LIST = 2
LANGS = 4
ROWS = 1024
SEQ = 4096
DOCS = 64


def draw_queries(key, part):
    drawn = jax.random.normal(jax.random.fold_in(key, 1), (SEQ, H * DH), jnp.float32)
    return jnp.clip(drawn, -6.0, 6.0).astype(jnp.bfloat16)


def draw_keys(key, part):
    drawn = jax.random.normal(jax.random.fold_in(key, 3), (SEQ, G * DH), jnp.float32)
    return jnp.clip(drawn, -6.0, 6.0).astype(jnp.bfloat16)


def draw_tile_list(key, part):
    tile_total = SEQ // BLOCK
    tiles_block = ROWS // BLOCK
    query_tile = jnp.arange(tile_total, dtype=jnp.int32)
    lowest = jnp.maximum((query_tile // tiles_block - 1) * tiles_block, 0)
    spread = query_tile - lowest + 1
    random_bits = jax.random.randint(jax.random.fold_in(key, 31), (G, tile_total, LIST), 0, 1 << 30)
    chosen = lowest[None, :, None] + random_bits % spread[None, :, None]
    chosen = chosen.at[:, tile_total - 1, 0].set(tile_total - 1)
    return chosen.astype(jnp.int32)


def touch_ends(result, rng, least, high):
    place = [jax.random.randint(jax.random.fold_in(rng, axis), (), 0, length) for axis, length in enumerate(result.shape)]
    longest = result.shape.index(max(result.shape))
    neighbour = place[:longest] + [(place[longest] + 1) % result.shape[longest]] + place[longest + 1:]
    return result.at[tuple(place)].set(least).at[tuple(neighbour)].set(high)


def level_of(key, dims, pieces, low, high):
    def one(position, blocks):
        steps = jax.random.uniform(jax.random.fold_in(jax.random.fold_in(key, 6), position), (blocks,), jnp.float32, low / len(pieces), high / len(pieces))
        return jnp.repeat(jnp.exp(steps), dims[position] // blocks).reshape((-1,) + (1,) * (len(dims) - position - 1))

    gain = one(*pieces[0])
    for cut in pieces[1:]:
        gain = gain * one(*cut)
    return gain


def length_profile(number_of, total, reach, skew):
    weights = [(1 << 20) // math.isqrt(standing ** skew) + 1 for standing in range(2, number_of + 1)]
    rest, given = total - reach - (number_of - 1), [1] * (number_of - 1)
    while rest > 0:
        free = [i for i in range(number_of - 1) if given[i] < reach]
        mass, remaining = sum([weights[i] for i in free]), rest
        for i in free:
            extra = min(reach - given[i], max(1, remaining * weights[i] // mass), rest)
            given[i] = given[i] + extra
            rest = rest - extra
    return np.array([reach] + given)


def uneven_parts(key, count, total, limit, slope):
    if count == 2:
        one = jax.random.randint(key, (), max(1, total - limit), min(limit, total - 1) + 1)
        return jnp.stack([one, total - one])
    sizes = jnp.asarray(length_profile(count, total, limit, slope), jnp.int32)
    couples = (count - 1) // 2
    donor, sink = sizes[1:1 + 2 * couples:2], sizes[2:2 + 2 * couples:2]
    margin = jnp.minimum(donor - 1, limit - sink)
    moved = jax.random.randint(jax.random.fold_in(key, 1), (couples,), 0, 1 << 20) % (margin + 1)
    sizes = sizes.at[1:1 + 2 * couples:2].set(donor - moved).at[2:2 + 2 * couples:2].set(sink + moved)
    return sizes[jax.random.permutation(jax.random.fold_in(key, 2), count)]


def noise(key, extent, width, reach, pieces=(), held_as=jnp.bfloat16):
    values = width * jax.random.normal(key, extent, jnp.float32)
    if pieces:
        values = values * level_of(key, extent, pieces, -0.22, 0.18)
    return jnp.clip(values, -reach, reach).astype(held_as)


def setup_inputs(seed: int = 0) -> dict:
    splits = jax.random.split(jax.random.key(seed), 9)
    queries = draw_queries(jax.random.fold_in(splits[8], 71), 0)
    keys = draw_keys(jax.random.fold_in(splits[8], 71), 0)
    values = noise(splits[2], (SEQ, G * DH), 1.0, 6.0, ((0, 32),))
    grad_out = noise(splits[3], (SEQ, H * DH), 1.0, 6.0, ((0, 32),))
    row_delta = noise(splits[4], (SEQ, H), 3.0, 18.0, ((0, 32),), jnp.float32)
    doc_ids = jnp.searchsorted(jnp.cumsum(uneven_parts(splits[5], DOCS, SEQ, BLOCK, 1)), jnp.arange(SEQ), side="right").astype(jnp.int32)
    doc_lang = touch_ends(jax.random.randint(splits[6], (DOCS,), 0, LANGS), jax.random.fold_in(splits[6], 1), 0, LANGS - 1).astype(jnp.int32)
    tile_list = draw_tile_list(jax.random.fold_in(splits[8], 71), 0)
    return dict(queries=queries, keys=keys, values=values, grad_out=grad_out, row_delta=row_delta, doc_ids=doc_ids, doc_lang=doc_lang, tile_list=tile_list)


MASKED = -1e30


def candidates(list_group, query_tiles):
    band_tiles = query_tiles[:, None] + jnp.arange(-1, 1, dtype=jnp.int32)[None, :]
    listed = jnp.take(list_group, query_tiles, axis=0, mode="clip")
    list_count = listed.shape[1]
    in_band = jnp.any(listed[:, :, None] == band_tiles[:, None, :], axis=2)
    earlier = jnp.tril(jnp.ones((list_count, list_count), jnp.bool_), -1)
    repeated = jnp.any((listed[:, :, None] == listed[:, None, :]) & earlier[None], axis=2)
    candidate = jnp.concatenate([band_tiles, listed], axis=1)
    usable = jnp.concatenate([band_tiles >= 0, jnp.logical_not(in_band | repeated)], axis=1)
    marked = jnp.any(candidate[:, :, None] == listed[:, None, :], axis=2)
    return candidate, usable, marked


def allowed_tiles(candidate, usable, marked, query_tiles, doc_ids, position_lang):
    offsets = jnp.arange(BLOCK, dtype=jnp.int32)
    query_pos = query_tiles[:, None] * BLOCK + offsets[None, :]
    key_pos = jnp.maximum(candidate, 0)[:, :, None] * BLOCK + offsets[None, None, :]
    query_doc = jnp.take(doc_ids, query_pos, mode="clip")
    key_doc = jnp.take(doc_ids, key_pos, mode="clip")
    query_lang = jnp.take(position_lang, query_pos, mode="clip")
    key_lang = jnp.take(position_lang, key_pos, mode="clip")
    causal = key_pos[:, :, None, :] <= query_pos[:, None, :, None]
    same_doc = key_doc[:, :, None, :] == query_doc[:, None, :, None]
    same_lang = key_lang[:, :, None, :] == query_lang[:, None, :, None]
    return usable[:, :, None, None] & causal & (same_doc | (same_lang & marked[:, :, None, None]))


def tile_setup(list_group, first_query, window_first, slot_count, tile_group, doc_ids, position_lang):
    query_tiles = first_query + jnp.arange(tile_group, dtype=jnp.int32)
    candidate, usable, marked = candidates(list_group, query_tiles)
    window_slot = candidate - window_first
    usable = usable & (window_slot >= 0) & (window_slot < slot_count)
    window_slot = jnp.clip(window_slot, 0, slot_count - 1)
    allowed = allowed_tiles(candidate, usable, marked, query_tiles, doc_ids, position_lang)
    return window_slot, allowed


def tile_stats(query_part, key_part, allowed, scaling):
    scores = scaling * jnp.einsum("qid,qcjd->qcij", query_part.astype(jnp.float32), key_part.astype(jnp.float32))
    masked = jnp.where(allowed, scores, MASKED)
    row_top = jnp.max(masked, axis=(1, 3))
    row_total = jnp.sum(jnp.where(allowed, jnp.exp(masked - row_top[:, None, :, None]), 0.0), axis=(1, 3))
    return row_top + jnp.log(row_total)


def tile_grads(query_part, dout_part, key_part, value_part, log_total, delta_part, allowed, scaling):
    scores = scaling * jnp.einsum("qid,qcjd->qcij", query_part.astype(jnp.float32), key_part.astype(jnp.float32))
    weights = jnp.where(allowed, jnp.exp(scores - log_total[:, None, :, None]), 0.0)
    weights_low = weights.astype(jnp.bfloat16)
    grad_value = jnp.einsum("qcij,qid->qcjd", weights_low.astype(jnp.float32), dout_part.astype(jnp.float32))
    grad_weights = jnp.einsum("qid,qcjd->qcij", dout_part.astype(jnp.float32), value_part.astype(jnp.float32))
    grad_scores = (weights * (grad_weights - delta_part[:, None, :, None])).astype(jnp.bfloat16)
    grad_query = scaling * jnp.einsum("qcij,qcjd->qid", grad_scores.astype(jnp.float32), key_part.astype(jnp.float32))
    grad_key = scaling * jnp.einsum("qcij,qid->qcjd", grad_scores.astype(jnp.float32), query_part.astype(jnp.float32))
    return grad_query, grad_key, grad_value


def stats_pass(query_one, key_tiles, list_group, first_tile, window_first, doc_ids, position_lang, tile_group, scaling):
    slot_count = key_tiles.shape[0]
    tile_count = query_one.shape[0] // BLOCK

    def stats_step(tile_start):
        window_slot, allowed = tile_setup(list_group, first_tile + tile_start, window_first, slot_count, tile_group,
                                          doc_ids, position_lang)
        query_part = lax.dynamic_slice_in_dim(query_one, tile_start * BLOCK, tile_group * BLOCK).reshape(tile_group, BLOCK, DH)
        key_part = jnp.take(key_tiles, window_slot, axis=0)
        return tile_stats(query_part, key_part, allowed, scaling)

    tile_starts = jnp.arange(tile_count // tile_group, dtype=jnp.int32) * tile_group
    return lax.map(stats_step, tile_starts).reshape(tile_count * BLOCK)


def grad_pass(query_one, dout_one, lse_one, delta_one, key_tiles, value_tiles, list_group, first_tile, window_first,
              doc_ids, position_lang, tile_group, scaling):
    slot_count = key_tiles.shape[0]
    tile_count = query_one.shape[0] // BLOCK

    def scan_step(carried, tile_start):
        key_sum, value_sum = carried
        window_slot, allowed = tile_setup(list_group, first_tile + tile_start, window_first, slot_count, tile_group,
                                          doc_ids, position_lang)
        row_start = tile_start * BLOCK
        row_span = tile_group * BLOCK
        query_part = lax.dynamic_slice_in_dim(query_one, row_start, row_span).reshape(tile_group, BLOCK, DH)
        dout_part = lax.dynamic_slice_in_dim(dout_one, row_start, row_span).reshape(tile_group, BLOCK, DH)
        lse_part = lax.dynamic_slice_in_dim(lse_one, row_start, row_span).reshape(tile_group, BLOCK)
        delta_part = lax.dynamic_slice_in_dim(delta_one, row_start, row_span).reshape(tile_group, BLOCK)
        key_part = jnp.take(key_tiles, window_slot, axis=0)
        value_part = jnp.take(value_tiles, window_slot, axis=0)
        grad_query, grad_key, grad_value = tile_grads(query_part, dout_part, key_part, value_part, lse_part, delta_part,
                                                      allowed, scaling)
        flat_slot = window_slot.reshape(-1)
        key_sum = key_sum.at[flat_slot].add(grad_key.reshape(-1, BLOCK, DH))
        value_sum = value_sum.at[flat_slot].add(grad_value.reshape(-1, BLOCK, DH))
        return (key_sum, value_sum), grad_query

    zero_tiles = jnp.zeros((slot_count, BLOCK, DH), jnp.float32)
    tile_starts = jnp.arange(tile_count // tile_group, dtype=jnp.int32) * tile_group
    sums, grad_query = lax.scan(scan_step, (zero_tiles, zero_tiles), tile_starts)
    return grad_query.reshape(-1, DH), sums[0].reshape(-1, DH), sums[1].reshape(-1, DH)


def reference(queries, keys, values, grad_out, row_delta, doc_ids, doc_lang, tile_list):
    seq_count = queries.shape[0]
    repeat_count = H // G
    scaling = float(DH) ** -0.5
    tile_total = seq_count // BLOCK
    tile_group = math.gcd(tile_total, 32)
    position_lang = jnp.take(doc_lang, doc_ids, mode="clip").astype(jnp.int32)

    def key_head(group_id):
        key_one = lax.dynamic_slice_in_dim(keys, group_id * DH, DH, axis=1)
        value_one = lax.dynamic_slice_in_dim(values, group_id * DH, DH, axis=1)
        list_group = lax.dynamic_index_in_dim(tile_list, group_id, 0, keepdims=False)
        key_tiles = key_one.reshape(tile_total, BLOCK, DH)
        value_tiles = value_one.reshape(tile_total, BLOCK, DH)
        key_total = jnp.zeros((seq_count, DH), jnp.float32)
        value_total = jnp.zeros((seq_count, DH), jnp.float32)
        query_grads = []
        for member in range(repeat_count):
            head = group_id * repeat_count + member
            query_one = lax.dynamic_slice_in_dim(queries, head * DH, DH, axis=1)
            dout_one = lax.dynamic_slice_in_dim(grad_out, head * DH, DH, axis=1)
            delta_one = lax.dynamic_index_in_dim(row_delta, head, 1, keepdims=False)
            zero_index = jnp.zeros((), jnp.int32)
            log_total = stats_pass(query_one, key_tiles, list_group, zero_index, zero_index, doc_ids, position_lang,
                                   tile_group, scaling)
            grad_query, head_key, head_value = grad_pass(query_one, dout_one, log_total, delta_one, key_tiles, value_tiles,
                                                         list_group, zero_index, zero_index, doc_ids, position_lang,
                                                         tile_group, scaling)
            key_total = key_total + lax.optimization_barrier(head_key.astype(jnp.bfloat16)).astype(jnp.float32)
            value_total = value_total + lax.optimization_barrier(head_value.astype(jnp.bfloat16)).astype(jnp.float32)
            query_grads.append(grad_query.astype(jnp.bfloat16))
        return jnp.stack(query_grads), key_total.astype(jnp.bfloat16), value_total.astype(jnp.bfloat16)

    grad_query, grad_key, grad_value = lax.map(key_head, jnp.arange(G, dtype=jnp.int32))
    grad_queries = grad_query.transpose(2, 0, 1, 3).reshape(seq_count, H * DH)
    grad_keys = grad_key.transpose(1, 0, 2).reshape(seq_count, G * DH)
    grad_values = grad_value.transpose(1, 0, 2).reshape(seq_count, G * DH)
    return grad_queries, grad_keys, grad_values
```

```python
import functools

import jax
import jax.numpy as jnp
from jax import lax
from jax.experimental import pallas as pl
from jax.experimental.pallas import tpu as pltpu
from jax.sharding import PartitionSpec as P

DH = 128
BLOCK = 128
LANGS = 4
MASKED = -1e30
MESH = pl.DeviceIdType.MESH
VMEM_LIMIT = 56 * 1024 * 1024


def greet(b, u, n_blk, n_uly):
    barrier = pltpu.get_barrier_semaphore()
    for p in range(1, n_uly):
        pl.semaphore_signal(
            barrier, inc=1, device_id=(b, lax.rem(u + p, n_uly)), device_id_type=MESH
        )

    @pl.when(b > 0)
    def _():
        pl.semaphore_signal(barrier, inc=1, device_id=(b - 1, u), device_id_type=MESH)

    @pl.when(b < n_blk - 1)
    def _():
        pl.semaphore_signal(barrier, inc=1, device_id=(b + 1, u), device_id_type=MESH)

    ends = jnp.where(b > 0, 1, 0) + jnp.where(b < n_blk - 1, 1, 0)
    pl.semaphore_wait(barrier, n_uly - 1 + ends)


def aligned(start, size):
    return pl.ds(pl.multiple_of(start, size), size)


def gather_kernel(
    n_blk,
    n_uly,
    heads_here,
    repeat_count,
    q_ref,
    do_ref,
    k_ref,
    v_ref,
    dl_ref,
    qo_ref,
    doo_ref,
    kw_ref,
    vw_ref,
    dlo_ref,
    send_sem,
    recv_sem,
    z_send,
    z_recv,
    local_sem,
):
    b, u = lax.axis_index("blk"), lax.axis_index("uly")
    tok = q_ref.shape[0]
    rows = tok * n_uly
    width = heads_here * DH
    mine = aligned(u * tok, tok)
    window_mine = aligned(rows + u * tok, tok)

    def pieces(peer):
        group = lax.div(peer * heads_here, repeat_count)
        kv_cols = aligned(group * DH, DH)
        q_cols = aligned(peer * width, width)
        return (
            (k_ref.at[:, kv_cols], kw_ref.at[window_mine, :]),
            (v_ref.at[:, kv_cols], vw_ref.at[window_mine, :]),
            (dl_ref.at[peer], dlo_ref.at[u]),
            (q_ref.at[:, q_cols], qo_ref.at[mine, :]),
            (do_ref.at[:, q_cols], doo_ref.at[mine, :]),
        )

    def remote(kind, p):
        peer = lax.rem(u + p, n_uly)
        src, dst = pieces(peer)[kind]
        return pltpu.make_async_remote_copy(
            src_ref=src,
            dst_ref=dst,
            send_sem=send_sem.at[kind, p],
            recv_sem=recv_sem.at[kind, p],
            device_id=(b, peer),
            device_id_type=MESH,
        )

    def local(kind):
        src, dst = pieces(u)[kind]
        return pltpu.make_async_copy(src, dst, local_sem.at[kind])

    def forward(kind):
        ref = (kw_ref, vw_ref)[kind]
        return pltpu.make_async_remote_copy(
            src_ref=ref.at[pl.ds(rows, rows), :],
            dst_ref=ref.at[pl.ds(0, rows), :],
            send_sem=z_send.at[kind],
            recv_sem=z_recv.at[kind],
            device_id=(lax.rem(b + 1, n_blk), u),
            device_id_type=MESH,
        )

    for kind in range(5):
        local(kind).start()
    greet(b, u, n_blk, n_uly)
    for kind in (0, 1):
        for p in range(1, n_uly):
            remote(kind, p).start()
    for p in range(1, n_uly):
        for kind in (2, 3, 4):
            remote(kind, p).start()
    for kind in (0, 1):
        local(kind).wait()
        for p in range(1, n_uly):
            remote(kind, p).wait_recv()

        @pl.when(b < n_blk - 1)
        def _():
            forward(kind).start()

    for kind in (2, 3, 4):
        local(kind).wait()
        for p in range(1, n_uly):
            remote(kind, p).wait_recv()
    for kind in range(5):
        for p in range(1, n_uly):
            remote(kind, p).wait_send()
    for kind in (0, 1):

        @pl.when(b < n_blk - 1)
        def _():
            forward(kind).wait_send()

        @pl.when(b > 0)
        def _():
            forward(kind).wait_recv()


def gathered(queries, grad_out, keys, values, delta_rows, n_blk, n_uly, repeat_count):
    tok_count, full_width = queries.shape
    rows = tok_count * n_uly
    width = full_width // n_uly
    heads_here = width // DH
    anywhere = pl.BlockSpec(memory_space=pl.ANY)
    bf16 = jnp.bfloat16
    return pl.pallas_call(
        functools.partial(gather_kernel, n_blk, n_uly, heads_here, repeat_count),
        out_shape=(
            jax.ShapeDtypeStruct((rows, width), bf16),
            jax.ShapeDtypeStruct((rows, width), bf16),
            jax.ShapeDtypeStruct((2 * rows, DH), bf16),
            jax.ShapeDtypeStruct((2 * rows, DH), bf16),
            jax.ShapeDtypeStruct((n_uly, heads_here, tok_count), jnp.float32),
        ),
        in_specs=[anywhere] * 5,
        out_specs=(anywhere,) * 5,
        scratch_shapes=[
            pltpu.SemaphoreType.DMA((5, n_uly)),
            pltpu.SemaphoreType.DMA((5, n_uly)),
            pltpu.SemaphoreType.DMA((2,)),
            pltpu.SemaphoreType.DMA((2,)),
            pltpu.SemaphoreType.DMA((5,)),
        ],
        compiler_params=pltpu.CompilerParams(collective_id=0, has_side_effects=True),
        name="gather_heads",
    )(queries, grad_out, keys, values, delta_rows)


def grads_kernel(
    tiles_here,
    tile_total,
    list_count,
    heads_here,
    repeat_count,
    list_ref,
    q_ref,
    do_ref,
    dl_ref,
    kw_ref,
    vw_ref,
    code_ref,
    dq_ref,
    back_ref,
    own_ref,
    key_codes,
    acc,
):
    a = pl.program_id(0)
    b, u = lax.axis_index("blk"), lax.axis_index("uly")
    rows = tiles_here * BLOCK
    scaling = float(DH) ** (-0.5)

    @pl.when(a == 0)
    def _():
        acc[...] = jnp.zeros_like(acc)

        @pl.loop(0, 2 * tiles_here)
        def _(t):
            row = jnp.broadcast_to(code_ref[pl.ds(t, 1), :], (BLOCK, BLOCK))
            key_codes[t] = row.T

    group = lax.div(u * heads_here, repeat_count)
    tile = b * tiles_here + a
    base = (group * tile_total + tile) * list_count
    listed = [list_ref[base + l] for l in range(list_count)]
    cands = [tile - 1, tile] + listed
    own_slot = tiles_here + a
    window_first = (b - 1) * tiles_here
    query_code = code_ref[pl.ds(own_slot, 1), :]
    query_lang = query_code & (LANGS - 1)
    gap = lax.broadcasted_iota(jnp.int32, (BLOCK, BLOCK), 0) - lax.broadcasted_iota(
        jnp.int32, (BLOCK, BLOCK), 1
    )
    slots = []
    biases = []
    for c, cand in enumerate(cands):
        usable = cand >= 0
        for other in cands[: c if c >= 2 else 0]:
            usable = usable & (cand != other)
        marked = cand == listed[0]
        for other in listed[1:]:
            marked = marked | (cand == other)
        slot = jnp.clip(cand - window_first, 0, 2 * tiles_here - 1)
        slot = jnp.where(usable, slot, own_slot)
        limit = jnp.where(usable, (tile - cand) * BLOCK, -2 * BLOCK)
        seen_lang = jnp.where(marked, query_lang, -1)
        key_code = key_codes[slot]
        allowed = (gap <= limit) & (
            (key_code == query_code) | ((key_code & (LANGS - 1)) == seen_lang)
        )
        slots.append(aligned(slot * BLOCK, BLOCK))
        biases.append(jnp.where(allowed, 0.0, MASKED))

    def stacked(ref):
        return jnp.concatenate([ref[:, h * DH : (h + 1) * DH] for h in range(heads_here)], axis=0)

    across = (((1,), (1,)), ((), ()))
    f32 = jnp.float32
    bias = jnp.concatenate(biases, axis=0)
    bias = jnp.concatenate([bias] * heads_here, axis=1)
    key_part = jnp.concatenate([kw_ref[s, :] for s in slots], axis=0)
    value_part = jnp.concatenate([vw_ref[s, :] for s in slots], axis=0)
    query_part = stacked(q_ref)
    dout_part = stacked(do_ref)
    delta = jnp.concatenate([dl_ref[0, h : h + 1, :] for h in range(heads_here)], axis=1)
    scores = lax.dot_general(key_part, query_part, across, preferred_element_type=f32)
    scores = scores * scaling + bias
    top = jnp.max(scores, axis=0, keepdims=True)
    raised = jnp.exp(scores - top)
    weights = raised * (1.0 / jnp.sum(raised, axis=0, keepdims=True))
    grad_weights = lax.dot_general(value_part, dout_part, across, preferred_element_type=f32)
    grad_scores = (weights * (grad_weights - delta)).astype(jnp.bfloat16)
    grad_value = jnp.dot(weights.astype(jnp.bfloat16), dout_part, preferred_element_type=f32)
    grad_key = scaling * jnp.dot(grad_scores, query_part, preferred_element_type=f32)
    grad_query = scaling * lax.dot_general(
        grad_scores, key_part, (((0,), (0,)), ((), ())), preferred_element_type=f32
    )
    for h in range(heads_here):
        dq_ref[:, h * DH : (h + 1) * DH] = grad_query[h * BLOCK : (h + 1) * BLOCK].astype(
            dq_ref.dtype
        )
    for c, s in enumerate(slots):
        acc[0, s, :] += grad_key[c * BLOCK : (c + 1) * BLOCK]
        acc[1, s, :] += grad_value[c * BLOCK : (c + 1) * BLOCK]

    @pl.when(a == tiles_here - 1)
    def _():
        back_ref[...] = acc[:, :rows, :].astype(back_ref.dtype)
        own_ref[...] = acc[:, rows:, :]


def grads(lists, query_heads, dout_heads, delta_heads, key_window, value_window, codes, sizes):
    tiles_here, tile_total, list_count, heads_here, repeat_count = sizes
    rows, width = query_heads.shape
    whole = pl.BlockSpec(memory_space=pltpu.VMEM)
    tile_spec = pl.BlockSpec((BLOCK, width), lambda a: (a, 0))
    flops = 5 * 2 * DH * rows * heads_here * (2 + list_count) * BLOCK
    return pl.pallas_call(
        functools.partial(grads_kernel, *sizes),
        grid=(tiles_here,),
        out_shape=(
            jax.ShapeDtypeStruct((rows, width), jnp.bfloat16),
            jax.ShapeDtypeStruct((2, rows, DH), jnp.bfloat16),
            jax.ShapeDtypeStruct((2, rows, DH), jnp.float32),
        ),
        in_specs=[
            pl.BlockSpec(memory_space=pltpu.SMEM),
            tile_spec,
            tile_spec,
            pl.BlockSpec((1, heads_here, BLOCK), lambda a: (a, 0, 0)),
            whole,
            whole,
            whole,
        ],
        out_specs=(
            tile_spec,
            pl.BlockSpec((2, rows, DH), lambda a: (0, 0, 0)),
            pl.BlockSpec((2, rows, DH), lambda a: (0, 0, 0)),
        ),
        scratch_shapes=[
            pltpu.VMEM((2 * tiles_here, BLOCK, BLOCK), jnp.int32),
            pltpu.VMEM((2, 2 * rows, DH), jnp.float32),
        ],
        compiler_params=pltpu.CompilerParams(
            dimension_semantics=("arbitrary",), vmem_limit_bytes=VMEM_LIMIT
        ),
        cost_estimate=pl.CostEstimate(
            flops=flops, bytes_accessed=12 * rows * width, transcendentals=flops // (10 * DH)
        ),
        name="tile_grads",
    )(lists, query_heads, dout_heads, delta_heads, key_window, value_window, codes)


def scatter_kernel(
    n_blk,
    n_uly,
    heads_here,
    repeat_count,
    dqh_ref,
    back_ref,
    own_ref,
    dq_ref,
    dk_ref,
    dv_ref,
    returned,
    total,
    landing,
    send_sem,
    recv_sem,
    z_send,
    z_recv,
    local_sem,
):
    b, u = lax.axis_index("blk"), lax.axis_index("uly")
    tok = dq_ref.shape[0]
    width = heads_here * DH
    copies = repeat_count // heads_here
    direct = copies == 1
    my_cols = aligned(u * width, width)
    my_group = aligned(u * DH, DH)

    def pieces(peer):
        theirs = aligned(peer * tok, tok)
        if direct:
            ends = (dk_ref.at[:, my_group], dv_ref.at[:, my_group])
        else:
            ends = (landing.at[0, u], landing.at[1, u])
        return (
            (total.at[0, theirs, :], ends[0]),
            (total.at[1, theirs, :], ends[1]),
            (dqh_ref.at[theirs, :], dq_ref.at[:, my_cols]),
        )

    def remote(kind, p):
        peer = lax.rem(u + p, n_uly)
        src, dst = pieces(peer)[kind]
        return pltpu.make_async_remote_copy(
            src_ref=src,
            dst_ref=dst,
            send_sem=send_sem.at[kind, p],
            recv_sem=recv_sem.at[kind, p],
            device_id=(b, peer),
            device_id_type=MESH,
        )

    def local(kind):
        src, dst = pieces(u)[kind]
        return pltpu.make_async_copy(src, dst, local_sem.at[kind])

    def backward(kind):
        return pltpu.make_async_remote_copy(
            src_ref=back_ref.at[kind],
            dst_ref=returned.at[kind],
            send_sem=z_send.at[kind],
            recv_sem=z_recv.at[kind],
            device_id=(lax.rem(b + n_blk - 1, n_blk), u),
            device_id_type=MESH,
        )

    local(2).start()
    greet(b, u, n_blk, n_uly)

    for kind in (0, 1):

        @pl.when(b > 0)
        def _():
            backward(kind).start()

    for p in range(1, n_uly):
        remote(2, p).start()

    for kind in (0, 1):

        @pl.when(b < n_blk - 1)
        def _():
            backward(kind).wait_recv()
            total[kind] = (own_ref[kind] + returned[kind].astype(jnp.float32)).astype(total.dtype)

        @pl.when(b == n_blk - 1)
        def _():
            total[kind] = own_ref[kind].astype(total.dtype)

        local(kind).start()
        for p in range(1, n_uly):
            remote(kind, p).start()

    for kind in (0, 1, 2):
        local(kind).wait()
        for p in range(1, n_uly):
            remote(kind, p).wait_recv()
    if not direct:
        for kind, out in ((0, dk_ref), (1, dv_ref)):
            for g in range(n_uly // copies):
                summed = landing[kind, g * copies].astype(jnp.float32)
                for r in range(1, copies):
                    summed = summed + landing[kind, g * copies + r].astype(jnp.float32)
                out[:, g * DH : (g + 1) * DH] = summed.astype(out.dtype)
    for kind in (0, 1, 2):
        for p in range(1, n_uly):
            remote(kind, p).wait_send()
    for kind in (0, 1):

        @pl.when(b > 0)
        def _():
            backward(kind).wait_send()


def scattered(dq_heads, back, own, n_blk, n_uly, repeat_count):
    rows, width = dq_heads.shape
    tok_count = rows // n_uly
    heads_here = width // DH
    copies = repeat_count // heads_here
    groups_all = n_uly // copies
    bf16 = jnp.bfloat16
    anywhere = pl.BlockSpec(memory_space=pl.ANY)
    in_vmem = pl.BlockSpec(memory_space=pltpu.VMEM)
    landing_count = n_uly if copies > 1 else 1
    kv_spec = in_vmem if copies > 1 else anywhere
    return pl.pallas_call(
        functools.partial(scatter_kernel, n_blk, n_uly, heads_here, repeat_count),
        out_shape=(
            jax.ShapeDtypeStruct((tok_count, width * n_uly), bf16),
            jax.ShapeDtypeStruct((tok_count, groups_all * DH), bf16),
            jax.ShapeDtypeStruct((tok_count, groups_all * DH), bf16),
        ),
        in_specs=[anywhere, anywhere, in_vmem],
        out_specs=(anywhere, kv_spec, kv_spec),
        scratch_shapes=[
            pltpu.VMEM((2, rows, DH), bf16),
            pltpu.VMEM((2, rows, DH), bf16),
            pltpu.VMEM((2, landing_count, tok_count, DH), bf16),
            pltpu.SemaphoreType.DMA((3, n_uly)),
            pltpu.SemaphoreType.DMA((3, n_uly)),
            pltpu.SemaphoreType.DMA((2,)),
            pltpu.SemaphoreType.DMA((2,)),
            pltpu.SemaphoreType.DMA((3,)),
        ],
        compiler_params=pltpu.CompilerParams(
            collective_id=1, has_side_effects=True, vmem_limit_bytes=VMEM_LIMIT
        ),
        name="scatter_tokens",
    )(dq_heads, back, own)


def window_codes(doc_ids, doc_lang, row_count):
    block_index = lax.axis_index("blk")
    earlier = lax.dynamic_slice_in_dim(
        doc_ids, jnp.maximum(block_index - 1, 0) * row_count, row_count
    )
    here = lax.dynamic_slice_in_dim(doc_ids, block_index * row_count, row_count)
    docs = jnp.concatenate([earlier, here]).reshape(-1, BLOCK)
    numbers = jnp.arange(doc_lang.shape[0], dtype=jnp.int32)
    hit = docs[None] == numbers[:, None, None]
    lang = jnp.sum(jnp.where(hit, doc_lang[:, None, None], 0), axis=0)
    return docs * LANGS + lang


def shards(queries, keys, values, grad_out, row_delta, doc_ids, doc_lang, tile_list):
    tok_count, full_width = queries.shape
    heads_all = full_width // DH
    groups_all = keys.shape[1] // DH
    repeat_count = heads_all // groups_all
    n_uly = lax.axis_size("uly")
    n_blk = lax.axis_size("blk")
    heads_here = heads_all // n_uly
    row_count = tok_count * n_uly
    sizes = (
        row_count // BLOCK,
        tile_list.shape[1],
        tile_list.shape[2],
        heads_here,
        repeat_count,
    )
    delta_rows = row_delta.T.reshape(n_uly, heads_here, tok_count)
    codes = window_codes(doc_ids, doc_lang, row_count)
    query_heads, dout_heads, key_window, value_window, delta_heads = gathered(
        queries, grad_out, keys, values, delta_rows, n_blk, n_uly, repeat_count
    )
    dq_heads, back, own = grads(
        tile_list.reshape(-1),
        query_heads,
        dout_heads,
        delta_heads,
        key_window,
        value_window,
        codes,
        sizes,
    )
    return scattered(dq_heads, back, own, n_blk, n_uly, repeat_count)


def solution(mesh):
    placed = (
        P(("blk", "uly"), None),
        P(("blk", "uly"), None),
        P(("blk", "uly"), None),
        P(("blk", "uly"), None),
        P(("blk", "uly"), None),
        P(),
        P(),
        P(),
    )
    return jax.shard_map(
        shards,
        mesh=mesh,
        in_specs=placed,
        out_specs=(P(("blk", "uly"), None), P(("blk", "uly"), None), P(("blk", "uly"), None)),
        check_vma=False,
    )
```

```python
import functools

import jax
import jax.numpy as jnp
from jax import lax
from jax.experimental import pallas as pl
from jax.experimental.pallas import tpu as pltpu
from jax.sharding import PartitionSpec as P

DH = 128
BLOCK = 128
LANGS = 4
MASKED = -1e30
MESH = pl.DeviceIdType.MESH
LOOK = 7
VMEM_LIMIT = 56 * 1024 * 1024


def greet(b, u, n_blk, n_uly):
    barrier = pltpu.get_barrier_semaphore()
    for p in range(1, n_uly):
        pl.semaphore_signal(
            barrier, inc=1, device_id=(b, lax.rem(u + p, n_uly)), device_id_type=MESH
        )

    @pl.when(b > 0)
    def _():
        pl.semaphore_signal(barrier, inc=1, device_id=(b - 1, u), device_id_type=MESH)

    @pl.when(b < n_blk - 1)
    def _():
        pl.semaphore_signal(barrier, inc=1, device_id=(b + 1, u), device_id_type=MESH)

    ends = jnp.where(b > 0, 1, 0) + jnp.where(b < n_blk - 1, 1, 0)
    pl.semaphore_wait(barrier, n_uly - 1 + ends)


def aligned(start, size):
    return pl.ds(pl.multiple_of(start, size), size)


def partner(u, s, n):
    s = jnp.where(s == 3, 4, jnp.where(s == 4, 3, s)) if n > 4 else s
    found, bit = 0, 1
    while bit < n:
        found = found + bit * lax.rem(lax.div(u, bit) + lax.div(s, bit), 2)
        bit *= 2
    return found


def fused_kernel(
    n_blk,
    n_uly,
    tile_total,
    list_count,
    heads_here,
    repeat_count,
    list_ref,
    q_ref,
    do_ref,
    k_ref,
    v_ref,
    dl_ref,
    code_ref,
    dq_ref,
    dk_ref,
    dv_ref,
    q_all,
    do_all,
    dl_all,
    window,
    key_codes,
    acc,
    dq_all,
    back,
    returned,
    total,
    landing,
    in_send,
    in_recv,
    local_sem,
    z_send,
    z_recv,
    back_send,
    back_recv,
    out_send,
    out_recv,
    out_local,
):
    b, u = lax.axis_index("blk"), lax.axis_index("uly")
    tiles_here = n_uly
    width = heads_here * DH
    copies = repeat_count // heads_here
    direct = copies == 1
    f32 = jnp.float32
    my_cols = aligned(u * width, width)
    my_group = aligned(u * DH, DH)
    peer_of = functools.partial(partner, u, n=n_uly)

    def pieces(peer):
        group = lax.div(peer * heads_here, repeat_count)
        kv_cols = aligned(group * DH, DH)
        q_cols = aligned(peer * width, width)
        return (
            (k_ref.at[:, kv_cols], window.at[tiles_here + u, 0]),
            (v_ref.at[:, kv_cols], window.at[tiles_here + u, 1]),
            (dl_ref.at[peer], dl_all.at[u]),
            (q_ref.at[:, q_cols], q_all.at[u]),
            (do_ref.at[:, q_cols], do_all.at[u]),
        )

    def out_pieces(peer):
        if direct:
            ends = (dk_ref.at[:, my_group], dv_ref.at[:, my_group])
        else:
            ends = (landing.at[0, u], landing.at[1, u])
        return (
            (total.at[peer, 0], ends[0]),
            (total.at[peer, 1], ends[1]),
            (dq_all.at[peer], dq_ref.at[:, my_cols]),
        )

    def remote(parts, kind, s, send, recv):
        peer = peer_of(s)
        src, dst = parts(peer)[kind]
        return pltpu.make_async_remote_copy(
            src_ref=src,
            dst_ref=dst,
            send_sem=send.at[kind, s],
            recv_sem=recv.at[kind, s],
            device_id=(b, peer),
            device_id_type=MESH,
        )

    def inward(kind, s):
        return remote(pieces, kind, s, in_send, in_recv)

    def outward(kind, s):
        return remote(out_pieces, kind, s, out_send, out_recv)

    def local(kind):
        src, dst = pieces(u)[kind]
        return pltpu.make_async_copy(src, dst, local_sem.at[kind])

    def out_own(kind):
        src, dst = out_pieces(u)[kind]
        return pltpu.make_async_copy(src, dst, out_local.at[kind])

    def forward(a):
        return pltpu.make_async_remote_copy(
            src_ref=window.at[tiles_here + a],
            dst_ref=window.at[a],
            send_sem=z_send.at[a],
            recv_sem=z_recv.at[a],
            device_id=(lax.rem(b + 1, n_blk), u),
            device_id_type=MESH,
        )

    def backward(a):
        return pltpu.make_async_remote_copy(
            src_ref=back.at[a],
            dst_ref=returned.at[a],
            send_sem=back_send.at[a],
            recv_sem=back_recv.at[a],
            device_id=(lax.rem(b + n_blk - 1, n_blk), u),
            device_id_type=MESH,
        )

    def each(first, last, body):
        lax.fori_loop(first, last, lambda s, _: (body(s), 0)[1], 0)

    has_next = b < n_blk - 1
    has_prev = b > 0

    for kind in range(5):
        local(kind).start()
    greet(b, u, n_blk, n_uly)

    def send_keys(s):
        inward(0, s).start()
        inward(1, s).start()

    def send_rows(s):
        inward(2, s).start()
        inward(3, s).start()
        inward(4, s).start()

    each(1, n_uly, send_keys)
    each(1, min(LOOK, n_uly - 1) + 1, send_rows)
    local(0).wait()
    local(1).wait()

    @pl.when(has_next)
    def _():
        forward(u).start()

    def prepare(t):
        key_codes[t] = jnp.broadcast_to(code_ref[pl.ds(t, 1), :], (BLOCK, BLOCK)).T
        acc[t] = jnp.zeros(acc.shape[1:], f32)

    each(0, 2 * tiles_here, prepare)

    @pl.when(b == 0)
    def _():
        window[0:tiles_here] = jnp.zeros((tiles_here,) + window.shape[1:], window.dtype)

    def pass_on(s):
        inward(0, s).wait_recv()
        inward(1, s).wait_recv()

        @pl.when(has_next)
        def _():
            forward(peer_of(s)).start()

    each(1, n_uly, pass_on)

    @pl.when(has_prev)
    def _():
        each(0, tiles_here, lambda a: forward(a).wait_recv())

    local(2).wait()
    local(3).wait()
    local(4).wait()

    scaling = float(DH) ** (-0.5)
    across = (((1,), (1,)), ((), ()))
    gap = lax.broadcasted_iota(jnp.int32, (BLOCK, BLOCK), 0) - lax.broadcasted_iota(
        jnp.int32, (BLOCK, BLOCK), 1
    )
    group_here = lax.div(u * heads_here, repeat_count)

    def tile_work(a):
        tile = b * tiles_here + a
        base = (group_here * tile_total + tile) * list_count
        listed = [list_ref[base + l] for l in range(list_count)]
        cands = [tile - 1, tile] + listed
        own_slot = tiles_here + a
        window_first = (b - 1) * tiles_here
        query_code = code_ref[pl.ds(own_slot, 1), :]
        query_lang = query_code & (LANGS - 1)
        slots = []
        biases = []
        for c, cand in enumerate(cands):
            usable = cand >= 0
            for other in cands[: c if c >= 2 else 0]:
                usable = usable & (cand != other)
            marked = cand == listed[0]
            for other in listed[1:]:
                marked = marked | (cand == other)
            if c < 2:
                slot = own_slot - 1 + c
            else:
                slot = jnp.clip(cand - window_first, 0, 2 * tiles_here - 1)
            limit = jnp.where(usable, (tile - cand) * BLOCK, -2 * BLOCK)
            seen_lang = jnp.where(marked, query_lang, -1)
            key_code = key_codes[slot]
            allowed = (gap <= limit) & (
                (key_code == query_code) | ((key_code & (LANGS - 1)) == seen_lang)
            )
            slots.append(slot)
            biases.append(jnp.where(allowed, 0.0, MASKED))

        def stacked(rows):
            return jnp.concatenate([rows[:, h * DH : (h + 1) * DH] for h in range(heads_here)], 0)

        bias = jnp.concatenate(biases, axis=0)
        bias = jnp.concatenate([bias] * heads_here, axis=1)
        key_part = jnp.concatenate([window[s, 0] for s in slots], axis=0)
        value_part = jnp.concatenate([window[s, 1] for s in slots], axis=0)
        query_part = stacked(q_all[a])
        dout_part = stacked(do_all[a])
        delta_tile = dl_all[a]
        delta = jnp.concatenate([delta_tile[h : h + 1, :] for h in range(heads_here)], axis=1)
        scores = lax.dot_general(key_part, query_part, across, preferred_element_type=f32)
        scores = scores * scaling + bias
        top = jnp.max(scores, axis=0, keepdims=True)
        raised = jnp.exp(scores - top)
        weights = raised * (1.0 / jnp.sum(raised, axis=0, keepdims=True))
        grad_weights = lax.dot_general(value_part, dout_part, across, preferred_element_type=f32)
        grad_scores = (weights * (grad_weights - delta)).astype(jnp.bfloat16)
        grad_query = scaling * lax.dot_general(
            grad_scores, key_part, (((0,), (0,)), ((), ())), preferred_element_type=f32
        )
        for h in range(heads_here):
            dq_all[a, :, h * DH : (h + 1) * DH] = grad_query[h * BLOCK : (h + 1) * BLOCK].astype(
                dq_all.dtype
            )
        grad_key = scaling * jnp.dot(grad_scores, query_part, preferred_element_type=f32)
        grad_value = jnp.dot(weights.astype(jnp.bfloat16), dout_part, preferred_element_type=f32)
        parts = (grad_key, grad_value)
        for c in range(2):
            for k in range(2):
                acc[slots[c], k] += parts[k][c * BLOCK : (c + 1) * BLOCK]

        def spread(t):
            for k in range(2):
                more = acc[t, k]
                for c in range(2, 2 + list_count):
                    piece = parts[k][c * BLOCK : (c + 1) * BLOCK]
                    more = more + jnp.where(slots[c] == t, piece, 0.0)
                acc[t, k] = more

        each(0, 2 * tiles_here, spread)

    tile_work(u)
    out_own(2).start()

    def step(s):
        @pl.when(s + LOOK < n_uly)
        def _():
            send_rows(s + LOOK)

        inward(2, s).wait_recv()
        inward(3, s).wait_recv()
        inward(4, s).wait_recv()
        tile_work(peer_of(s))
        outward(2, s).start()

    each(1, n_uly, step)

    @pl.when(has_prev)
    def _():
        def give_back(s):
            a = peer_of(s)
            back[a] = acc[a].astype(back.dtype)
            backward(a).start()

        each(0, n_uly, give_back)

    def settle(s):
        a = peer_of(s)

        @pl.when(has_next)
        def _():
            backward(a).wait_recv()
            total[a] = (acc[tiles_here + a] + returned[a].astype(f32)).astype(total.dtype)

        @pl.when(b == n_blk - 1)
        def _():
            total[a] = acc[tiles_here + a].astype(total.dtype)

    settle(0)
    out_own(0).start()
    out_own(1).start()

    def settle_and_send(s):
        settle(s)
        outward(0, s).start()
        outward(1, s).start()

    each(1, n_uly, settle_and_send)

    for kind in range(3):
        out_own(kind).wait()

    def finish(s):
        for kind in range(3):
            outward(kind, s).wait_recv()
        for kind in range(5):
            inward(kind, s).wait_send()
        for kind in range(3):
            outward(kind, s).wait_send()

    each(1, n_uly, finish)

    @pl.when(has_next)
    def _():
        each(0, n_uly, lambda a: forward(a).wait_send())

    @pl.when(has_prev)
    def _():
        each(0, n_uly, lambda a: backward(a).wait_send())

    if not direct:
        for kind, out in ((0, dk_ref), (1, dv_ref)):
            for g in range(n_uly // copies):
                summed = landing[kind, g * copies].astype(f32)
                for r in range(1, copies):
                    summed = summed + landing[kind, g * copies + r].astype(f32)
                out[:, g * DH : (g + 1) * DH] = summed.astype(out.dtype)


def window_codes(doc_ids, doc_lang, row_count):
    block_index = lax.axis_index("blk")
    earlier = lax.dynamic_slice_in_dim(
        doc_ids, jnp.maximum(block_index - 1, 0) * row_count, row_count
    )
    here = lax.dynamic_slice_in_dim(doc_ids, block_index * row_count, row_count)
    docs = jnp.concatenate([earlier, here]).reshape(-1, BLOCK)
    numbers = jnp.arange(doc_lang.shape[0], dtype=jnp.int32)
    hit = docs[None] == numbers[:, None, None]
    lang = jnp.sum(jnp.where(hit, doc_lang[:, None, None], 0), axis=0)
    return docs * LANGS + lang


def shards(queries, keys, values, grad_out, row_delta, doc_ids, doc_lang, tile_list):
    tok_count, full_width = queries.shape
    heads_all = full_width // DH
    groups_all = keys.shape[1] // DH
    repeat_count = heads_all // groups_all
    n_uly = lax.axis_size("uly")
    n_blk = lax.axis_size("blk")
    heads_here = heads_all // n_uly
    width = heads_here * DH
    copies = repeat_count // heads_here
    row_count = tok_count * n_uly
    delta_rows = row_delta.T.reshape(n_uly, heads_here, tok_count)
    codes = window_codes(doc_ids, doc_lang, row_count)
    anywhere = pl.BlockSpec(memory_space=pl.ANY)
    in_vmem = pl.BlockSpec(memory_space=pltpu.VMEM)
    kv_spec = in_vmem if copies > 1 else anywhere
    bf16, f32 = jnp.bfloat16, jnp.float32
    pair = (2, BLOCK, DH)
    dma = pltpu.SemaphoreType.DMA
    return pl.pallas_call(
        functools.partial(
            fused_kernel,
            n_blk,
            n_uly,
            tile_list.shape[1],
            tile_list.shape[2],
            heads_here,
            repeat_count,
        ),
        out_shape=(
            jax.ShapeDtypeStruct(queries.shape, bf16),
            jax.ShapeDtypeStruct(keys.shape, bf16),
            jax.ShapeDtypeStruct(values.shape, bf16),
        ),
        in_specs=[pl.BlockSpec(memory_space=pltpu.SMEM)] + [anywhere] * 5 + [in_vmem],
        out_specs=(anywhere, kv_spec, kv_spec),
        scratch_shapes=[
            pltpu.VMEM((n_uly, BLOCK, width), bf16),
            pltpu.VMEM((n_uly, BLOCK, width), bf16),
            pltpu.VMEM((n_uly, heads_here, BLOCK), f32),
            pltpu.VMEM((2 * n_uly,) + pair, bf16),
            pltpu.VMEM((2 * n_uly, BLOCK, BLOCK), jnp.int32),
            pltpu.VMEM((2 * n_uly,) + pair, f32),
            pltpu.VMEM((n_uly, BLOCK, width), bf16),
            pltpu.VMEM((n_uly,) + pair, bf16),
            pltpu.VMEM((n_uly,) + pair, bf16),
            pltpu.VMEM((n_uly,) + pair, bf16),
            pltpu.VMEM((2, n_uly if copies > 1 else 1, BLOCK, DH), bf16),
            dma((5, n_uly)),
            dma((5, n_uly)),
            dma((5,)),
            dma((n_uly,)),
            dma((n_uly,)),
            dma((n_uly,)),
            dma((n_uly,)),
            dma((3, n_uly)),
            dma((3, n_uly)),
            dma((3,)),
        ],
        compiler_params=pltpu.CompilerParams(
            collective_id=0, has_side_effects=True, vmem_limit_bytes=VMEM_LIMIT
        ),
        name="attention_grads",
    )(tile_list.reshape(-1), queries, grad_out, keys, values, delta_rows, codes)


def solution(mesh):
    placed = (
        P(("blk", "uly"), None),
        P(("blk", "uly"), None),
        P(("blk", "uly"), None),
        P(("blk", "uly"), None),
        P(("blk", "uly"), None),
        P(),
        P(),
        P(),
    )
    return jax.shard_map(
        shards,
        mesh=mesh,
        in_specs=placed,
        out_specs=(P(("blk", "uly"), None), P(("blk", "uly"), None), P(("blk", "uly"), None)),
        check_vma=False,
    )
```

```python
import functools

import jax
import jax.numpy as jnp
from jax import lax
from jax.experimental import pallas as pl
from jax.experimental.pallas import tpu as pltpu
from jax.sharding import PartitionSpec as P

DH = 128
BLOCK = 128
LANGS = 4
MASKED = -1e30
MESH = pl.DeviceIdType.MESH
LOOK = 7
VMEM_LIMIT = 56 * 1024 * 1024


def greet(b, u, n_blk, n_uly):
    barrier = pltpu.get_barrier_semaphore()
    for p in range(1, n_uly):
        pl.semaphore_signal(
            barrier, inc=1, device_id=(b, lax.rem(u + p, n_uly)), device_id_type=MESH
        )

    @pl.when(b > 0)
    def _():
        pl.semaphore_signal(barrier, inc=1, device_id=(b - 1, u), device_id_type=MESH)

    @pl.when(b < n_blk - 1)
    def _():
        pl.semaphore_signal(barrier, inc=1, device_id=(b + 1, u), device_id_type=MESH)

    ends = jnp.where(b > 0, 1, 0) + jnp.where(b < n_blk - 1, 1, 0)
    pl.semaphore_wait(barrier, n_uly - 1 + ends)


def aligned(start, size):
    return pl.ds(pl.multiple_of(start, size), size)


def partner(u, s, n):
    s = jnp.where(s == 3, 4, jnp.where(s == 4, 3, s)) if n > 4 else s
    found, bit = 0, 1
    while bit < n:
        found = found + bit * lax.rem(lax.div(u, bit) + lax.div(s, bit), 2)
        bit *= 2
    return found


def fused_kernel(
    n_blk,
    n_uly,
    list_count,
    heads_here,
    repeat_count,
    list_hbm,
    lang_hbm,
    docs_hbm,
    q_ref,
    do_ref,
    k_ref,
    v_ref,
    dl_ref,
    dq_ref,
    dk_ref,
    dv_ref,
    q_all,
    do_all,
    dl_all,
    window,
    list_ref,
    lang_ref,
    code_ref,
    key_codes,
    acc,
    dq_all,
    back,
    returned,
    total,
    landing,
    in_send,
    in_recv,
    local_sem,
    z_send,
    z_recv,
    back_send,
    back_recv,
    out_send,
    out_recv,
    out_local,
    table_sem,
):
    b, u = lax.axis_index("blk"), lax.axis_index("uly")
    tiles_here = n_uly
    width = heads_here * DH
    copies = repeat_count // heads_here
    direct = copies == 1
    f32 = jnp.float32
    my_cols = aligned(u * width, width)
    my_group = aligned(u * DH, DH)
    peer_of = functools.partial(partner, u, n=n_uly)

    def pieces(peer):
        group = lax.div(peer * heads_here, repeat_count)
        kv_cols = aligned(group * DH, DH)
        q_cols = aligned(peer * width, width)
        return (
            (k_ref.at[:, kv_cols], window.at[tiles_here + u, 0]),
            (v_ref.at[:, kv_cols], window.at[tiles_here + u, 1]),
            (dl_ref.at[peer], dl_all.at[u]),
            (q_ref.at[:, q_cols], q_all.at[u]),
            (do_ref.at[:, q_cols], do_all.at[u]),
        )

    def out_pieces(peer):
        if direct:
            ends = (dk_ref.at[:, my_group], dv_ref.at[:, my_group])
        else:
            ends = (landing.at[0, u], landing.at[1, u])
        return (
            (total.at[peer, 0], ends[0]),
            (total.at[peer, 1], ends[1]),
            (dq_all.at[peer], dq_ref.at[:, my_cols]),
        )

    def remote(parts, kind, s, send, recv):
        peer = peer_of(s)
        src, dst = parts(peer)[kind]
        return pltpu.make_async_remote_copy(
            src_ref=src,
            dst_ref=dst,
            send_sem=send.at[kind, s],
            recv_sem=recv.at[kind, s],
            device_id=(b, peer),
            device_id_type=MESH,
        )

    def inward(kind, s):
        return remote(pieces, kind, s, in_send, in_recv)

    def outward(kind, s):
        return remote(out_pieces, kind, s, out_send, out_recv)

    def local(kind):
        src, dst = pieces(u)[kind]
        return pltpu.make_async_copy(src, dst, local_sem.at[kind])

    def out_own(kind):
        src, dst = out_pieces(u)[kind]
        return pltpu.make_async_copy(src, dst, out_local.at[kind])

    def forward(a):
        return pltpu.make_async_remote_copy(
            src_ref=window.at[tiles_here + a],
            dst_ref=window.at[a],
            send_sem=z_send.at[a],
            recv_sem=z_recv.at[a],
            device_id=(lax.rem(b + 1, n_blk), u),
            device_id_type=MESH,
        )

    def backward(a):
        return pltpu.make_async_remote_copy(
            src_ref=back.at[a],
            dst_ref=returned.at[a],
            send_sem=back_send.at[a],
            recv_sem=back_recv.at[a],
            device_id=(lax.rem(b + n_blk - 1, n_blk), u),
            device_id_type=MESH,
        )

    def each(first, last, body):
        lax.fori_loop(first, last, lambda s, _: (body(s), 0)[1], 0)

    has_next = b < n_blk - 1
    has_prev = b > 0

    tables = (
        pltpu.make_async_copy(list_hbm, list_ref, table_sem.at[0]),
        pltpu.make_async_copy(lang_hbm, lang_ref, table_sem.at[1]),
        pltpu.make_async_copy(
            docs_hbm.at[aligned(jnp.maximum(b - 1, 0) * tiles_here, tiles_here), :],
            code_ref.at[pl.ds(0, tiles_here), :],
            table_sem.at[2],
        ),
        pltpu.make_async_copy(
            docs_hbm.at[aligned(b * tiles_here, tiles_here), :],
            code_ref.at[pl.ds(tiles_here, tiles_here), :],
            table_sem.at[3],
        ),
    )
    for kind in range(5):
        local(kind).start()
    for table in tables:
        table.start()
    greet(b, u, n_blk, n_uly)

    def send_keys(s):
        inward(0, s).start()
        inward(1, s).start()

    def send_rows(s):
        inward(2, s).start()
        inward(3, s).start()
        inward(4, s).start()

    each(1, n_uly, send_keys)
    each(1, min(LOOK, n_uly - 1) + 1, send_rows)
    local(0).wait()
    local(1).wait()

    @pl.when(has_next)
    def _():
        forward(u).start()

    for table in tables:
        table.wait()
    docs = code_ref[...]

    def look_up(d, lang):
        return lang + jnp.where(docs == d, lang_ref[d], 0)

    lang = lax.fori_loop(0, lang_ref.shape[0], look_up, jnp.zeros_like(docs))
    code_ref[...] = docs * LANGS + lang

    def prepare(t):
        key_codes[t] = jnp.broadcast_to(code_ref[pl.ds(t, 1), :], (BLOCK, BLOCK)).T
        acc[t] = jnp.zeros(acc.shape[1:], f32)

    each(0, 2 * tiles_here, prepare)

    @pl.when(b == 0)
    def _():
        window[0:tiles_here] = jnp.zeros((tiles_here,) + window.shape[1:], window.dtype)

    def pass_on(s):
        inward(0, s).wait_recv()
        inward(1, s).wait_recv()

        @pl.when(has_next)
        def _():
            forward(peer_of(s)).start()

    each(1, n_uly, pass_on)

    @pl.when(has_prev)
    def _():
        each(0, tiles_here, lambda a: forward(a).wait_recv())

    local(2).wait()
    local(3).wait()
    local(4).wait()

    scaling = float(DH) ** (-0.5)
    across = (((1,), (1,)), ((), ()))
    gap = lax.broadcasted_iota(jnp.int32, (BLOCK, BLOCK), 0) - lax.broadcasted_iota(
        jnp.int32, (BLOCK, BLOCK), 1
    )
    group_here = lax.div(u * heads_here, repeat_count)

    def tile_work(a):
        tile = b * tiles_here + a
        listed = [list_ref[group_here, l, tile] for l in range(list_count)]
        cands = [tile - 1, tile] + listed
        own_slot = tiles_here + a
        window_first = (b - 1) * tiles_here
        query_code = code_ref[pl.ds(own_slot, 1), :]
        query_lang = query_code & (LANGS - 1)
        slots = []
        biases = []
        for c, cand in enumerate(cands):
            usable = cand >= 0
            for other in cands[: c if c >= 2 else 0]:
                usable = usable & (cand != other)
            marked = cand == listed[0]
            for other in listed[1:]:
                marked = marked | (cand == other)
            if c < 2:
                slot = own_slot - 1 + c
            else:
                slot = jnp.clip(cand - window_first, 0, 2 * tiles_here - 1)
            limit = jnp.where(usable, (tile - cand) * BLOCK, -2 * BLOCK)
            seen_lang = jnp.where(marked, query_lang, -1)
            key_code = key_codes[slot]
            allowed = (gap <= limit) & (
                (key_code == query_code) | ((key_code & (LANGS - 1)) == seen_lang)
            )
            slots.append(slot)
            biases.append(jnp.where(allowed, 0.0, MASKED))

        def stacked(rows):
            return jnp.concatenate([rows[:, h * DH : (h + 1) * DH] for h in range(heads_here)], 0)

        bias = jnp.concatenate(biases, axis=0)
        bias = jnp.concatenate([bias] * heads_here, axis=1)
        key_part = jnp.concatenate([window[s, 0] for s in slots], axis=0)
        value_part = jnp.concatenate([window[s, 1] for s in slots], axis=0)
        query_part = stacked(q_all[a])
        dout_part = stacked(do_all[a])
        delta_tile = dl_all[a]
        delta = jnp.concatenate([delta_tile[h : h + 1, :] for h in range(heads_here)], axis=1)
        scores = lax.dot_general(key_part, query_part, across, preferred_element_type=f32)
        scores = scores * scaling + bias
        top = jnp.max(scores, axis=0, keepdims=True)
        raised = jnp.exp(scores - top)
        weights = raised * (1.0 / jnp.sum(raised, axis=0, keepdims=True))
        grad_weights = lax.dot_general(value_part, dout_part, across, preferred_element_type=f32)
        grad_scores = (weights * (grad_weights - delta)).astype(jnp.bfloat16)
        grad_query = scaling * lax.dot_general(
            grad_scores, key_part, (((0,), (0,)), ((), ())), preferred_element_type=f32
        )
        for h in range(heads_here):
            dq_all[a, :, h * DH : (h + 1) * DH] = grad_query[h * BLOCK : (h + 1) * BLOCK].astype(
                dq_all.dtype
            )
        grad_key = scaling * jnp.dot(grad_scores, query_part, preferred_element_type=f32)
        grad_value = jnp.dot(weights.astype(jnp.bfloat16), dout_part, preferred_element_type=f32)
        parts = (grad_key, grad_value)
        for c in range(2):
            for k in range(2):
                acc[slots[c], k] += parts[k][c * BLOCK : (c + 1) * BLOCK]

        def spread(t):
            for k in range(2):
                more = acc[t, k]
                for c in range(2, 2 + list_count):
                    piece = parts[k][c * BLOCK : (c + 1) * BLOCK]
                    more = more + jnp.where(slots[c] == t, piece, 0.0)
                acc[t, k] = more

        each(0, 2 * tiles_here, spread)

    tile_work(u)
    out_own(2).start()

    def step(s):
        @pl.when(s + LOOK < n_uly)
        def _():
            send_rows(s + LOOK)

        inward(2, s).wait_recv()
        inward(3, s).wait_recv()
        inward(4, s).wait_recv()
        tile_work(peer_of(s))
        outward(2, s).start()

    each(1, n_uly, step)

    @pl.when(has_prev)
    def _():
        def give_back(s):
            a = peer_of(s)
            back[a] = acc[a].astype(back.dtype)
            backward(a).start()

        each(0, n_uly, give_back)

    def settle(s):
        a = peer_of(s)

        @pl.when(has_next)
        def _():
            backward(a).wait_recv()
            total[a] = (acc[tiles_here + a] + returned[a].astype(f32)).astype(total.dtype)

        @pl.when(b == n_blk - 1)
        def _():
            total[a] = acc[tiles_here + a].astype(total.dtype)

    settle(0)
    out_own(0).start()
    out_own(1).start()

    def settle_and_send(s):
        settle(s)
        outward(0, s).start()
        outward(1, s).start()

    each(1, n_uly, settle_and_send)

    for kind in range(3):
        out_own(kind).wait()

    def finish(s):
        for kind in range(3):
            outward(kind, s).wait_recv()
        for kind in range(5):
            inward(kind, s).wait_send()
        for kind in range(3):
            outward(kind, s).wait_send()

    each(1, n_uly, finish)

    @pl.when(has_next)
    def _():
        each(0, n_uly, lambda a: forward(a).wait_send())

    @pl.when(has_prev)
    def _():
        each(0, n_uly, lambda a: backward(a).wait_send())

    if not direct:
        for kind, out in ((0, dk_ref), (1, dv_ref)):
            for g in range(n_uly // copies):
                summed = landing[kind, g * copies].astype(f32)
                for r in range(1, copies):
                    summed = summed + landing[kind, g * copies + r].astype(f32)
                out[:, g * DH : (g + 1) * DH] = summed.astype(out.dtype)


def hand_over_kernel(*refs):
    count = len(refs) // 2
    sems = refs[-1]
    moves = []
    for k in range(count):
        src, dst = refs[k], refs[count + k]
        half = src.shape[0] // 2
        for part in range(2):
            rows = pl.ds(part * half, half)
            moves.append(
                pltpu.make_async_copy(src.at[rows, :], dst.at[rows, :], sems.at[2 * k + part])
            )
    for move in moves:
        move.start()
    for move in moves:
        move.wait()


def handed_over(arrays):
    anywhere = pl.BlockSpec(memory_space=pl.ANY)
    return pl.pallas_call(
        hand_over_kernel,
        out_shape=tuple(jax.ShapeDtypeStruct(x.shape, x.dtype) for x in arrays),
        in_specs=[anywhere] * len(arrays),
        out_specs=(anywhere,) * len(arrays),
        scratch_shapes=[pltpu.SemaphoreType.DMA((2 * len(arrays),))],
        name="hand_over",
    )(*arrays)


def copy_body(*refs):
    count = len(refs) // 2
    for k in range(count):
        refs[count + k][...] = refs[k][...]


def handed_over_v(arrays):
    specs = [pl.BlockSpec((64, x.shape[1]), lambda i: (i, 0)) for x in arrays]
    return pl.pallas_call(
        copy_body,
        grid=(arrays[0].shape[0] // 64,),
        out_shape=tuple(jax.ShapeDtypeStruct(x.shape, x.dtype) for x in arrays),
        in_specs=specs,
        out_specs=tuple(specs),
        name="hand_over",
    )(*arrays)


def shards(queries, keys, values, grad_out, row_delta, doc_ids, doc_lang, tile_list):
    tok_count, full_width = queries.shape
    heads_all = full_width // DH
    groups_all = keys.shape[1] // DH
    repeat_count = heads_all // groups_all
    n_uly = lax.axis_size("uly")
    n_blk = lax.axis_size("blk")
    heads_here = heads_all // n_uly
    width = heads_here * DH
    copies = repeat_count // heads_here
    lists = tile_list.transpose(0, 2, 1)
    docs = doc_ids.reshape(-1, BLOCK)
    delta_rows = row_delta.T.reshape(n_uly, heads_here, tok_count)
    anywhere = pl.BlockSpec(memory_space=pl.ANY)
    in_vmem = pl.BlockSpec(memory_space=pltpu.VMEM)
    kv_spec = in_vmem if copies > 1 else anywhere
    bf16, f32 = jnp.bfloat16, jnp.float32
    pair = (2, BLOCK, DH)
    dma = pltpu.SemaphoreType.DMA
    outs = pl.pallas_call(
        functools.partial(
            fused_kernel,
            n_blk,
            n_uly,
            tile_list.shape[2],
            heads_here,
            repeat_count,
        ),
        out_shape=(
            jax.ShapeDtypeStruct(queries.shape, bf16),
            jax.ShapeDtypeStruct(keys.shape, bf16),
            jax.ShapeDtypeStruct(values.shape, bf16),
        ),
        in_specs=[anywhere] * 8,
        out_specs=(anywhere, kv_spec, kv_spec),
        scratch_shapes=[
            pltpu.VMEM((n_uly, BLOCK, width), bf16),
            pltpu.VMEM((n_uly, BLOCK, width), bf16),
            pltpu.VMEM((n_uly, heads_here, BLOCK), f32),
            pltpu.VMEM((2 * n_uly,) + pair, bf16),
            pltpu.SMEM(lists.shape, jnp.int32),
            pltpu.SMEM(doc_lang.shape, jnp.int32),
            pltpu.VMEM((2 * n_uly, BLOCK), jnp.int32),
            pltpu.VMEM((2 * n_uly, BLOCK, BLOCK), jnp.int32),
            pltpu.VMEM((2 * n_uly,) + pair, f32),
            pltpu.VMEM((n_uly, BLOCK, width), bf16),
            pltpu.VMEM((n_uly,) + pair, bf16),
            pltpu.VMEM((n_uly,) + pair, bf16),
            pltpu.VMEM((n_uly,) + pair, bf16),
            pltpu.VMEM((2, n_uly if copies > 1 else 1, BLOCK, DH), bf16),
            dma((5, n_uly)),
            dma((5, n_uly)),
            dma((5,)),
            dma((n_uly,)),
            dma((n_uly,)),
            dma((n_uly,)),
            dma((n_uly,)),
            dma((3, n_uly)),
            dma((3, n_uly)),
            dma((3,)),
            dma((4,)),
        ],
        compiler_params=pltpu.CompilerParams(
            collective_id=0, has_side_effects=True, vmem_limit_bytes=VMEM_LIMIT
        ),
        name="attention_grads",
    )(lists, doc_lang, docs, queries, grad_out, keys, values, delta_rows)
    return handed_over_v(outs)


def solution(mesh):
    placed = (
        P(("blk", "uly"), None),
        P(("blk", "uly"), None),
        P(("blk", "uly"), None),
        P(("blk", "uly"), None),
        P(("blk", "uly"), None),
        P(),
        P(),
        P(),
    )
    return jax.shard_map(
        shards,
        mesh=mesh,
        in_specs=placed,
        out_specs=(P(("blk", "uly"), None), P(("blk", "uly"), None), P(("blk", "uly"), None)),
        check_vma=False,
    )
```

```python
import functools

import jax
import jax.numpy as jnp
from jax import lax
from jax.experimental import pallas as pl
from jax.experimental.pallas import tpu as pltpu
from jax.sharding import PartitionSpec as P

DH = 128
BLOCK = 128
LANGS = 4
MASKED = -1e30
MESH = pl.DeviceIdType.MESH
LOOK = 7
CHUNKS = 4
VMEM_LIMIT = 56 * 1024 * 1024


def greet(b, u, n_blk, n_uly):
    barrier = pltpu.get_barrier_semaphore()
    for p in range(1, n_uly):
        pl.semaphore_signal(
            barrier, inc=1, device_id=(b, lax.rem(u + p, n_uly)), device_id_type=MESH
        )

    @pl.when(b > 0)
    def _():
        pl.semaphore_signal(barrier, inc=1, device_id=(b - 1, u), device_id_type=MESH)

    @pl.when(b < n_blk - 1)
    def _():
        pl.semaphore_signal(barrier, inc=1, device_id=(b + 1, u), device_id_type=MESH)

    ends = jnp.where(b > 0, 1, 0) + jnp.where(b < n_blk - 1, 1, 0)
    pl.semaphore_wait(barrier, n_uly - 1 + ends)


def aligned(start, size):
    return pl.ds(pl.multiple_of(start, size), size)


def partner(u, s, n):
    found, bit = 0, 1
    while bit < n:
        found = found + bit * lax.rem(lax.div(u, bit) + lax.div(s, bit), 2)
        bit *= 2
    return found


def fused_kernel(
    n_blk,
    n_uly,
    list_count,
    heads_here,
    repeat_count,
    list_hbm,
    lang_hbm,
    docs_hbm,
    q_ref,
    do_ref,
    k_ref,
    v_ref,
    dl_ref,
    dq_ref,
    dk_ref,
    dv_ref,
    q_all,
    do_all,
    dl_all,
    window,
    list_ref,
    lang_ref,
    code_ref,
    key_codes,
    acc,
    dq_all,
    back,
    returned,
    total,
    landing,
    in_send,
    in_recv,
    local_sem,
    z_send,
    z_recv,
    back_send,
    back_recv,
    out_send,
    out_recv,
    out_local,
    table_sem,
):
    b, u = lax.axis_index("blk"), lax.axis_index("uly")
    tiles_here = n_uly
    width = heads_here * DH
    copies = repeat_count // heads_here
    direct = copies == 1
    f32 = jnp.float32
    my_cols = aligned(u * width, width)
    my_group = aligned(u * DH, DH)
    peer_of = functools.partial(partner, u, n=n_uly)

    def pieces(peer):
        group = lax.div(peer * heads_here, repeat_count)
        kv_cols = aligned(group * DH, DH)
        q_cols = aligned(peer * width, width)
        return (
            (k_ref.at[:, kv_cols], window.at[tiles_here + u, 0]),
            (v_ref.at[:, kv_cols], window.at[tiles_here + u, 1]),
            (dl_ref.at[peer], dl_all.at[u]),
            (q_ref.at[:, q_cols], q_all.at[u]),
            (do_ref.at[:, q_cols], do_all.at[u]),
        )

    def out_pieces(peer):
        if direct:
            ends = (dk_ref.at[:, my_group], dv_ref.at[:, my_group])
        else:
            ends = (landing.at[0, u], landing.at[1, u])
        return (
            (total.at[peer, 0], ends[0]),
            (total.at[peer, 1], ends[1]),
            (dq_all.at[peer], dq_ref.at[:, my_cols]),
        )

    def remote(parts, kind, s, send, recv):
        peer = peer_of(s)
        src, dst = parts(peer)[kind]
        return pltpu.make_async_remote_copy(
            src_ref=src,
            dst_ref=dst,
            send_sem=send.at[kind, s],
            recv_sem=recv.at[kind, s],
            device_id=(b, peer),
            device_id_type=MESH,
        )

    def inward(kind, s):
        return remote(pieces, kind, s, in_send, in_recv)

    def outward(kind, s):
        return remote(out_pieces, kind, s, out_send, out_recv)

    def local(kind):
        src, dst = pieces(u)[kind]
        return pltpu.make_async_copy(src, dst, local_sem.at[kind])

    def out_own(kind):
        src, dst = out_pieces(u)[kind]
        return pltpu.make_async_copy(src, dst, out_local.at[kind])

    def forward(a):
        return pltpu.make_async_remote_copy(
            src_ref=window.at[tiles_here + a],
            dst_ref=window.at[a],
            send_sem=z_send.at[a],
            recv_sem=z_recv.at[a],
            device_id=(lax.rem(b + 1, n_blk), u),
            device_id_type=MESH,
        )

    def backward(a):
        return pltpu.make_async_remote_copy(
            src_ref=back.at[a],
            dst_ref=returned.at[a],
            send_sem=back_send.at[a],
            recv_sem=back_recv.at[a],
            device_id=(lax.rem(b + n_blk - 1, n_blk), u),
            device_id_type=MESH,
        )

    def each(first, last, body):
        lax.fori_loop(first, last, lambda s, _: (body(s), 0)[1], 0)

    has_next = b < n_blk - 1
    has_prev = b > 0

    tables = (
        pltpu.make_async_copy(list_hbm, list_ref, table_sem.at[0]),
        pltpu.make_async_copy(lang_hbm, lang_ref, table_sem.at[1]),
        pltpu.make_async_copy(
            docs_hbm.at[aligned(jnp.maximum(b - 1, 0) * tiles_here, tiles_here), :],
            code_ref.at[pl.ds(0, tiles_here), :],
            table_sem.at[2],
        ),
        pltpu.make_async_copy(
            docs_hbm.at[aligned(b * tiles_here, tiles_here), :],
            code_ref.at[pl.ds(tiles_here, tiles_here), :],
            table_sem.at[3],
        ),
    )
    for kind in range(5):
        local(kind).start()
    for table in tables:
        table.start()
    greet(b, u, n_blk, n_uly)

    def send_keys(s):
        inward(0, s).start()
        inward(1, s).start()

    def send_rows(s):
        inward(2, s).start()
        inward(3, s).start()
        inward(4, s).start()

    each(1, n_uly, send_keys)
    each(1, min(LOOK, n_uly - 1) + 1, send_rows)
    local(0).wait()
    local(1).wait()

    @pl.when(has_next)
    def _():
        forward(u).start()

    for table in tables:
        table.wait()
    docs = code_ref[...]

    def look_up(d, lang):
        return lang + jnp.where(docs == d, lang_ref[d], 0)

    lang = lax.fori_loop(0, lang_ref.shape[0], look_up, jnp.zeros_like(docs))
    code_ref[...] = docs * LANGS + lang

    def prepare(t):
        key_codes[t] = jnp.broadcast_to(code_ref[pl.ds(t, 1), :], (BLOCK, BLOCK)).T
        acc[t] = jnp.zeros(acc.shape[1:], f32)

    each(0, 2 * tiles_here, prepare)

    @pl.when(b == 0)
    def _():
        window[0:tiles_here] = jnp.zeros((tiles_here,) + window.shape[1:], window.dtype)

    def pass_on(s):
        inward(0, s).wait_recv()
        inward(1, s).wait_recv()

        @pl.when(has_next)
        def _():
            forward(peer_of(s)).start()

    each(1, n_uly, pass_on)

    @pl.when(has_prev)
    def _():
        each(0, tiles_here, lambda a: forward(a).wait_recv())

    local(2).wait()
    local(3).wait()
    local(4).wait()

    scaling = float(DH) ** (-0.5)
    across = (((1,), (1,)), ((), ()))
    gap = lax.broadcasted_iota(jnp.int32, (BLOCK, BLOCK), 0) - lax.broadcasted_iota(
        jnp.int32, (BLOCK, BLOCK), 1
    )
    group_here = lax.div(u * heads_here, repeat_count)

    def tile_work(a):
        tile = b * tiles_here + a
        listed = [list_ref[group_here, l, tile] for l in range(list_count)]
        cands = [tile - 1, tile] + listed
        own_slot = tiles_here + a
        window_first = (b - 1) * tiles_here
        query_code = code_ref[pl.ds(own_slot, 1), :]
        query_lang = query_code & (LANGS - 1)
        slots = []
        biases = []
        for c, cand in enumerate(cands):
            usable = cand >= 0
            for other in cands[: c if c >= 2 else 0]:
                usable = usable & (cand != other)
            marked = cand == listed[0]
            for other in listed[1:]:
                marked = marked | (cand == other)
            if c < 2:
                slot = own_slot - 1 + c
            else:
                slot = jnp.clip(cand - window_first, 0, 2 * tiles_here - 1)
            limit = jnp.where(usable, (tile - cand) * BLOCK, -2 * BLOCK)
            seen_lang = jnp.where(marked, query_lang, -1)
            key_code = key_codes[slot]
            allowed = (gap <= limit) & (
                (key_code == query_code) | ((key_code & (LANGS - 1)) == seen_lang)
            )
            slots.append(slot)
            biases.append(jnp.where(allowed, 0.0, MASKED))

        def stacked(rows):
            return jnp.concatenate([rows[:, h * DH : (h + 1) * DH] for h in range(heads_here)], 0)

        bias = jnp.concatenate(biases, axis=0)
        bias = jnp.concatenate([bias] * heads_here, axis=1)
        key_part = jnp.concatenate([window[s, 0] for s in slots], axis=0)
        value_part = jnp.concatenate([window[s, 1] for s in slots], axis=0)
        query_part = stacked(q_all[a])
        dout_part = stacked(do_all[a])
        delta_tile = dl_all[a]
        delta = jnp.concatenate([delta_tile[h : h + 1, :] for h in range(heads_here)], axis=1)
        scores = lax.dot_general(key_part, query_part, across, preferred_element_type=f32)
        scores = scores * scaling + bias
        top = jnp.max(scores, axis=0, keepdims=True)
        raised = jnp.exp(scores - top)
        weights = raised * (1.0 / jnp.sum(raised, axis=0, keepdims=True))
        grad_weights = lax.dot_general(value_part, dout_part, across, preferred_element_type=f32)
        grad_scores = (weights * (grad_weights - delta)).astype(jnp.bfloat16)
        grad_query = scaling * lax.dot_general(
            grad_scores, key_part, (((0,), (0,)), ((), ())), preferred_element_type=f32
        )
        for h in range(heads_here):
            dq_all[a, :, h * DH : (h + 1) * DH] = grad_query[h * BLOCK : (h + 1) * BLOCK].astype(
                dq_all.dtype
            )
        grad_key = scaling * jnp.dot(grad_scores, query_part, preferred_element_type=f32)
        grad_value = jnp.dot(weights.astype(jnp.bfloat16), dout_part, preferred_element_type=f32)
        parts = (grad_key, grad_value)
        for c in range(2):
            for k in range(2):
                acc[slots[c], k] += parts[k][c * BLOCK : (c + 1) * BLOCK]

        def spread(t):
            for k in range(2):
                more = acc[t, k]
                for c in range(2, 2 + list_count):
                    piece = parts[k][c * BLOCK : (c + 1) * BLOCK]
                    more = more + jnp.where(slots[c] == t, piece, 0.0)
                acc[t, k] = more

        each(0, 2 * tiles_here, spread)

    tile_work(u)
    out_own(2).start()

    def step(s):
        @pl.when(s + LOOK < n_uly)
        def _():
            send_rows(s + LOOK)

        inward(2, s).wait_recv()
        inward(3, s).wait_recv()
        inward(4, s).wait_recv()
        tile_work(peer_of(s))
        outward(2, s).start()

    each(1, n_uly, step)

    @pl.when(has_prev)
    def _():
        def give_back(s):
            a = peer_of(s)
            back[a] = acc[a].astype(back.dtype)
            backward(a).start()

        each(0, n_uly, give_back)

    def settle(s):
        a = peer_of(s)

        @pl.when(has_next)
        def _():
            backward(a).wait_recv()
            total[a] = (acc[tiles_here + a] + returned[a].astype(f32)).astype(total.dtype)

        @pl.when(b == n_blk - 1)
        def _():
            total[a] = acc[tiles_here + a].astype(total.dtype)

    settle(0)
    out_own(0).start()
    out_own(1).start()

    def settle_and_send(s):
        settle(s)
        outward(0, s).start()
        outward(1, s).start()

    each(1, n_uly, settle_and_send)

    for kind in range(3):
        out_own(kind).wait()

    def finish(s):
        for kind in range(3):
            outward(kind, s).wait_recv()
        for kind in range(5):
            inward(kind, s).wait_send()
        for kind in range(3):
            outward(kind, s).wait_send()

    each(1, n_uly, finish)

    @pl.when(has_next)
    def _():
        each(0, n_uly, lambda a: forward(a).wait_send())

    @pl.when(has_prev)
    def _():
        each(0, n_uly, lambda a: backward(a).wait_send())

    if not direct:
        for kind, out in ((0, dk_ref), (1, dv_ref)):
            for g in range(n_uly // copies):
                summed = landing[kind, g * copies].astype(f32)
                for r in range(1, copies):
                    summed = summed + landing[kind, g * copies + r].astype(f32)
                out[:, g * DH : (g + 1) * DH] = summed.astype(out.dtype)


def hand_over_kernel(*refs):
    count = (len(refs) - 2) // 3
    in_sem, out_sem = refs[-2:]
    moves = []
    for k in range(count):
        src, dst, held = refs[k], refs[count + k], refs[2 * count + k]
        part = src.shape[0] // CHUNKS
        for c in range(CHUNKS):
            rows = pl.ds(c * part, part)
            moves.append(
                (
                    pltpu.make_async_copy(src.at[rows, :], held.at[rows, :], in_sem.at[k, c]),
                    pltpu.make_async_copy(held.at[rows, :], dst.at[rows, :], out_sem.at[k, c]),
                )
            )
    for fetch, _ in moves:
        fetch.start()
    for fetch, store in moves:
        fetch.wait()
        store.start()
    for _, store in moves:
        store.wait()


def handed_over(arrays):
    anywhere = pl.BlockSpec(memory_space=pl.ANY)
    count = len(arrays)
    return pl.pallas_call(
        hand_over_kernel,
        out_shape=tuple(jax.ShapeDtypeStruct(x.shape, x.dtype) for x in arrays),
        in_specs=[anywhere] * count,
        out_specs=(anywhere,) * count,
        scratch_shapes=[pltpu.VMEM(x.shape, x.dtype) for x in arrays]
        + [pltpu.SemaphoreType.DMA((count, CHUNKS)), pltpu.SemaphoreType.DMA((count, CHUNKS))],
        name="hand_over",
    )(*arrays)


def shards(queries, keys, values, grad_out, row_delta, doc_ids, doc_lang, tile_list):
    tok_count, full_width = queries.shape
    heads_all = full_width // DH
    groups_all = keys.shape[1] // DH
    repeat_count = heads_all // groups_all
    n_uly = lax.axis_size("uly")
    n_blk = lax.axis_size("blk")
    heads_here = heads_all // n_uly
    width = heads_here * DH
    copies = repeat_count // heads_here
    lists = tile_list.transpose(0, 2, 1)
    docs = doc_ids.reshape(-1, BLOCK)
    delta_rows = row_delta.T.reshape(n_uly, heads_here, tok_count)
    anywhere = pl.BlockSpec(memory_space=pl.ANY)
    in_vmem = pl.BlockSpec(memory_space=pltpu.VMEM)
    kv_spec = in_vmem if copies > 1 else anywhere
    bf16, f32 = jnp.bfloat16, jnp.float32
    pair = (2, BLOCK, DH)
    dma = pltpu.SemaphoreType.DMA
    outs = pl.pallas_call(
        functools.partial(
            fused_kernel,
            n_blk,
            n_uly,
            tile_list.shape[2],
            heads_here,
            repeat_count,
        ),
        out_shape=(
            jax.ShapeDtypeStruct(queries.shape, bf16),
            jax.ShapeDtypeStruct(keys.shape, bf16),
            jax.ShapeDtypeStruct(values.shape, bf16),
        ),
        in_specs=[anywhere] * 8,
        out_specs=(anywhere, kv_spec, kv_spec),
        scratch_shapes=[
            pltpu.VMEM((n_uly, BLOCK, width), bf16),
            pltpu.VMEM((n_uly, BLOCK, width), bf16),
            pltpu.VMEM((n_uly, heads_here, BLOCK), f32),
            pltpu.VMEM((2 * n_uly,) + pair, bf16),
            pltpu.SMEM(lists.shape, jnp.int32),
            pltpu.SMEM(doc_lang.shape, jnp.int32),
            pltpu.VMEM((2 * n_uly, BLOCK), jnp.int32),
            pltpu.VMEM((2 * n_uly, BLOCK, BLOCK), jnp.int32),
            pltpu.VMEM((2 * n_uly,) + pair, f32),
            pltpu.VMEM((n_uly, BLOCK, width), bf16),
            pltpu.VMEM((n_uly,) + pair, bf16),
            pltpu.VMEM((n_uly,) + pair, bf16),
            pltpu.VMEM((n_uly,) + pair, bf16),
            pltpu.VMEM((2, n_uly if copies > 1 else 1, BLOCK, DH), bf16),
            dma((5, n_uly)),
            dma((5, n_uly)),
            dma((5,)),
            dma((n_uly,)),
            dma((n_uly,)),
            dma((n_uly,)),
            dma((n_uly,)),
            dma((3, n_uly)),
            dma((3, n_uly)),
            dma((3,)),
            dma((4,)),
        ],
        compiler_params=pltpu.CompilerParams(
            collective_id=0, has_side_effects=True, vmem_limit_bytes=VMEM_LIMIT
        ),
        name="attention_grads",
    )(lists, doc_lang, docs, queries, grad_out, keys, values, delta_rows)
    return handed_over(outs)


def solution(mesh):
    placed = (
        P(("blk", "uly"), None),
        P(("blk", "uly"), None),
        P(("blk", "uly"), None),
        P(("blk", "uly"), None),
        P(("blk", "uly"), None),
        P(),
        P(),
        P(),
    )
    return jax.shard_map(
        shards,
        mesh=mesh,
        in_specs=placed,
        out_specs=(P(("blk", "uly"), None), P(("blk", "uly"), None), P(("blk", "uly"), None)),
        check_vma=False,
    )
```
